128 devices in a mesh: gx: 16 (over x, y_hi, core), gy: 8 (over y_lo, z).
Axes of the slice: x: 4, y: 4 (y_hi: 2, y_lo: 2; y = y_hi * 2 + y_lo), z: 4, core: 2. Of those that a mesh axis runs over, the one named last changes fastest.
Arguments:
- right_side: float32 [512, 256, 512], P('gx', 'gy'), may hold values from -24 to 24
- alpha_coef: float32 [512, 256, 512], P('gx', 'gy'), may hold values from 0.05 to 0.5
- face_coef: float32 [3, 512, 256, 512], P(None, 'gx', 'gy'), may hold values from 0.25 to 4
- owner_map: int32 [8, 256], P('gy'), may hold values from 0 to 15, as said below
Outputs:
- solution: float32 [512, 256, 512], P('gx', 'gy')
- coarse_residual: float32 [256, 128, 256], P('gx', 'gy')
- coarse_coef: float32 [4, 256, 128, 256], P(None, 'gx', 'gy')
The draws below stay inside these ranges and needn't reach their ends.
Inputs may be any that keep to these rules, and one draw needn't show every extreme that they name: `owner_map`: each row's tiles are cut by recursive bisection into boxes of 4 x 4 tiles, one box to each owner; every device that sends to an owner sends it exactly 4 tiles.
All inputs are finite; a program needn't handle non-finite values.
Results may differ from the reference program's by a relative error of at most 0.00002.
Values sent between devices are 32-bit elements; how exact they have to be, the bound alone decides.
A program may use at most 192 MiB of HBM per device.

```python
import math
import jax
import jax.numpy as jnp

SIDE = 4
ITERS = 4
TZ = 16
HALF = 16
NX = 512
NY = 256
NZ = 512
TILES = 256
N_GX = 16
N_GY = 8


def draw_owner_map(key, part):
    boxes_x = N_GX // SIDE
    extent_x = boxes_x
    extent_z = SIDE
    levels = []
    while extent_x * extent_z > 1:
        if extent_x >= extent_z:
            extent_x = extent_x // 2
            levels.append((0, extent_x))
        else:
            extent_z = extent_z // 2
            levels.append((1, extent_z))
    box_x = jnp.broadcast_to((jnp.arange(N_GX, dtype=jnp.int32) // SIDE)[:, None], (N_GX, TZ))
    box_z = jnp.broadcast_to((jnp.arange(TZ, dtype=jnp.int32) // SIDE)[None, :], (N_GX, TZ))
    label = jnp.zeros((N_GY, N_GX * TZ), jnp.int32)
    node_id = jnp.zeros((N_GY, N_GX * TZ), jnp.int32)
    for level_index, (split_dim, split_size) in enumerate(levels):
        coords = box_x if split_dim == 0 else box_z
        half_bit = (coords // split_size % 2).reshape(1, N_GX * TZ)
        flips = jax.random.randint(jax.random.fold_in(key, level_index + 11), (N_GY, 2 ** level_index), 0, 2).astype(jnp.int32)
        flip_bit = jnp.take_along_axis(flips, node_id, axis=1)
        label = label * 2 + (half_bit + flip_bit) % 2
        node_id = node_id * 2 + half_bit
    return label.astype(jnp.int32)


def block_levels(rng, shape, pieces, least, largest):
    def one(axis_at, parts):
        steps = jax.random.uniform(jax.random.fold_in(jax.random.fold_in(rng, 6), axis_at), (parts,), jnp.float32, least / len(pieces), largest / len(pieces))
        return jnp.repeat(jnp.exp(steps), shape[axis_at] // parts).reshape((-1,) + (1,) * (len(shape) - axis_at - 1))

    loudness = one(*pieces[0])
    for cut in pieces[1:]:
        loudness = loudness * one(*cut)
    return loudness


def scatter_about(rng, shape, scale, limit, shards=(), kind=jnp.bfloat16):
    entries = scale * jax.random.normal(rng, shape, jnp.float32)
    if shards:
        entries = entries * block_levels(rng, shape, shards, -0.22, 0.18)
    return jnp.clip(entries, -limit, limit).astype(kind)


def setup_inputs(seed: int = 0) -> dict:
    splits = jax.random.split(jax.random.key(seed), 5)
    right_side = scatter_about(splits[0], (NX, NY, NZ), 4.0, 24.0, ((0, 16), (1, 8)), jnp.float32)
    alpha_coef = jnp.clip(jnp.exp(math.log(0.5) - 2.3025851 * jax.random.uniform(splits[1], (NX, NY, NZ), jnp.float32) ** block_levels(splits[1], (NX, NY, NZ), ((0, 16), (1, 8)), -0.2, 0.2)), 0.05, 0.5)
    face_coef = jnp.clip(jnp.exp(math.log(4.0) - 2.7725887 * jax.random.uniform(splits[2], (3, NX, NY, NZ), jnp.float32) ** block_levels(splits[2], (3, NX, NY, NZ), ((1, 16), (2, 8)), -0.2, 0.2)), 0.25, 4.0)
    owner_map = draw_owner_map(jax.random.fold_in(splits[4], 71), 0)
    return {"right_side": right_side, "alpha_coef": alpha_coef, "face_coef": face_coef, "owner_map": owner_map}


cheb_high = 2.0
cheb_low = 0.25


def shift_lower(field):
    return jnp.concatenate([jnp.zeros_like(field[..., :1]), field[..., :-1]], axis=-1)


def shift_upper(field):
    return jnp.concatenate([field[..., 1:], jnp.zeros_like(field[..., :1])], axis=-1)


def apply_operator(padded, alpha_inner, faces_padded):
    center = padded[1:-1, 1:-1]
    face_x = faces_padded[0, 1:-1, 1:-1]
    face_xu = faces_padded[0, 2:, 1:-1]
    face_y = faces_padded[1, 1:-1, 1:-1]
    face_yu = faces_padded[1, 1:-1, 2:]
    face_z = faces_padded[2, 1:-1, 1:-1]
    face_zu = shift_upper(face_z)
    result = alpha_inner * center
    result = result + face_x * (center - padded[:-2, 1:-1]) + face_xu * (center - padded[2:, 1:-1])
    result = result + face_y * (center - padded[1:-1, :-2]) + face_yu * (center - padded[1:-1, 2:])
    result = result + face_z * (center - shift_lower(center)) + face_zu * (center - shift_upper(center))
    return result


def diagonal_of(alpha_inner, faces_padded):
    face_x = faces_padded[0, 1:-1, 1:-1]
    face_xu = faces_padded[0, 2:, 1:-1]
    face_y = faces_padded[1, 1:-1, 1:-1]
    face_yu = faces_padded[1, 1:-1, 2:]
    face_z = faces_padded[2, 1:-1, 1:-1]
    return alpha_inner + face_x + face_xu + face_y + face_yu + face_z + shift_upper(face_z)


def pad_cells(field):
    return jnp.pad(field, ((1, 1), (1, 1), (0, 0)))


def average_cells(field):
    shaped = field.reshape(field.shape[0] // 2, 2, field.shape[1] // 2, 2, field.shape[2] // 2, 2)
    return jnp.sum(shaped, axis=(1, 3, 5)) * 0.125


def average_faces(faces):
    shaped = faces.reshape(3, faces.shape[1] // 2, 2, faces.shape[2] // 2, 2, faces.shape[3] // 2, 2)
    along_x = jnp.sum(shaped[0][:, 0], axis=(2, 4)) * 0.25
    along_y = jnp.sum(shaped[1][:, :, :, 0], axis=(1, 4)) * 0.25
    along_z = jnp.sum(shaped[2][..., 0], axis=(1, 3)) * 0.25
    return [along_x, along_y, along_z]


def owner_tiles(coarse, order):
    shaped = coarse.reshape(N_GX, HALF, N_GY, HALF, TZ, HALF)
    tiles = shaped.transpose(2, 0, 4, 3, 1, 5).reshape(N_GY, TILES, HALF, HALF * HALF)
    ordered = jnp.take_along_axis(tiles, order[:, :, None, None], axis=1)
    return ordered.transpose(1, 0, 2, 3).reshape(TILES, N_GY * HALF, HALF * HALF)


def reference(right_side, alpha_coef, face_coef, owner_map):
    theta_mid = (cheb_high + cheb_low) / 2.0
    delta_half = (cheb_high - cheb_low) / 2.0
    sigma_ratio = theta_mid / delta_half
    faces_padded = jnp.pad(face_coef, ((0, 0), (1, 1), (1, 1), (0, 0)))
    inverse = 1.0 / diagonal_of(alpha_coef, faces_padded)
    solution = inverse * right_side / theta_mid
    update = solution
    rho_prev = 1.0 / sigma_ratio
    for _ in range(ITERS - 1):
        residual = right_side - apply_operator(pad_cells(solution), alpha_coef, faces_padded)
        rho_next = 1.0 / (2.0 * sigma_ratio - rho_prev)
        update = rho_next * rho_prev * update + (2.0 * rho_next / delta_half) * inverse * residual
        solution = solution + update
        rho_prev = rho_next
    residual = right_side - apply_operator(pad_cells(solution), alpha_coef, faces_padded)
    order = jnp.argsort(owner_map, axis=1, stable=True).astype(jnp.int32)
    coarse_residual = owner_tiles(average_cells(residual), order)
    fields = [average_cells(alpha_coef)] + average_faces(face_coef)
    coarse_coef = jnp.stack([owner_tiles(field, order) for field in fields])
    return solution, coarse_residual, coarse_coef
```

```python
import jax
import jax.numpy as jnp
from jax import lax
from jax.sharding import PartitionSpec as P

SIDE = 4
ITERS = 4


cheb_high = 2.0
cheb_low = 0.25


def padded_2(cells, sides, width):
    for axis, dim in sides:
        count = lax.axis_size(axis)
        ends = count - 1
        head = lax.slice_in_dim(cells, 0, width, axis=dim)
        tail = lax.slice_in_dim(cells, cells.shape[dim] - width, cells.shape[dim], axis=dim)
        cells = jnp.concatenate(
            [
                lax.ppermute(tail, axis, [(i, (i + 1) % count) for i in range(ends)]),
                cells,
                lax.ppermute(head, axis, [((i + 1) % count, i) for i in range(ends)]),
            ],
            axis=dim,
        )
    return cells


def passed_along(block, axis, distance):
    devices = range(lax.axis_size(axis))
    route = [(i - distance, i) for i in devices if i - distance in devices]
    return lax.ppermute(block, axis, route)


def shift_lower(field):
    return jnp.concatenate([jnp.zeros_like(field[..., :1]), field[..., :-1]], axis=-1)


def shift_upper(field):
    return jnp.concatenate([field[..., 1:], jnp.zeros_like(field[..., :1])], axis=-1)


def apply_operator(padded, alpha_inner, faces_padded):
    center = padded[1:-1, 1:-1]
    face_x = faces_padded[0, 1:-1, 1:-1]
    face_xu = faces_padded[0, 2:, 1:-1]
    face_y = faces_padded[1, 1:-1, 1:-1]
    face_yu = faces_padded[1, 1:-1, 2:]
    face_z = faces_padded[2, 1:-1, 1:-1]
    face_zu = shift_upper(face_z)
    result = alpha_inner * center
    result = result + face_x * (center - padded[:-2, 1:-1]) + face_xu * (center - padded[2:, 1:-1])
    result = result + face_y * (center - padded[1:-1, :-2]) + face_yu * (center - padded[1:-1, 2:])
    result = (
        result + face_z * (center - shift_lower(center)) + face_zu * (center - shift_upper(center))
    )
    return result


def diagonal_of(alpha_inner, faces_padded):
    face_x = faces_padded[0, 1:-1, 1:-1]
    face_xu = faces_padded[0, 2:, 1:-1]
    face_y = faces_padded[1, 1:-1, 1:-1]
    face_yu = faces_padded[1, 1:-1, 2:]
    face_z = faces_padded[2, 1:-1, 1:-1]
    return alpha_inner + face_x + face_xu + face_y + face_yu + face_z + shift_upper(face_z)


def chebyshev_constants():
    theta_mid = (cheb_high + cheb_low) / 2.0
    delta_half = (cheb_high - cheb_low) / 2.0
    return (theta_mid, delta_half, theta_mid / delta_half)


def field_with_rim(field):
    return padded_2(field, (("gx", 0), ("gy", 1)), 1)


def faces_with_next(face_coef):
    next_x = passed_along(face_coef[0, :1], "gx", -1)
    next_y = passed_along(face_coef[1, :, :1], "gy", -1)
    padded_x = jnp.pad(jnp.concatenate([face_coef[0], next_x], axis=0), ((1, 0), (1, 1), (0, 0)))
    padded_y = jnp.pad(jnp.concatenate([face_coef[1], next_y], axis=1), ((1, 1), (1, 0), (0, 0)))
    padded_z = jnp.pad(face_coef[2], ((1, 1), (1, 1), (0, 0)))
    return jnp.stack([padded_x, padded_y, padded_z], axis=0)


def smooth_each(right_side, alpha_coef, face_coef):
    theta_mid, delta_half, sigma_ratio = chebyshev_constants()
    faces_padded = faces_with_next(face_coef)
    inverse = 1.0 / diagonal_of(alpha_coef, faces_padded)
    solution = inverse * right_side / theta_mid
    update = solution
    rho_prev = 1.0 / sigma_ratio
    for _ in range(ITERS - 1):
        residual = right_side - apply_operator(field_with_rim(solution), alpha_coef, faces_padded)
        rho_next = 1.0 / (2.0 * sigma_ratio - rho_prev)
        update = rho_next * rho_prev * update + 2.0 * rho_next / delta_half * inverse * residual
        solution = solution + update
        rho_prev = rho_next
    residual = right_side - apply_operator(field_with_rim(solution), alpha_coef, faces_padded)
    return (solution, residual)


def z_matrix(cells, even_only):
    fine = lax.broadcasted_iota(jnp.int32, (cells, cells // 2), 0)
    coarse = lax.broadcasted_iota(jnp.int32, (cells, cells // 2), 1)
    hit = fine // 2 == coarse
    if even_only:
        hit = hit & (fine % 2 == 0)
    return hit.astype(jnp.float32)


def restrict_z(field, even_only=False):
    cells = field.shape[-1]
    flat = field.reshape(-1, cells)
    summed = jnp.dot(flat, z_matrix(cells, even_only), precision=lax.Precision.HIGHEST)
    return summed.reshape(field.shape[:-1] + (cells // 2,))


def split_major(field):
    return field.reshape(field.shape[0] // 2, 2, field.shape[1] // 2, 2, field.shape[2])


def average_cells(field):
    return restrict_z(jnp.sum(split_major(field), axis=(1, 3))) * 0.125


def average_faces(faces):
    along_x = restrict_z(jnp.sum(split_major(faces[0])[:, 0], axis=2)) * 0.25
    along_y = restrict_z(jnp.sum(split_major(faces[1])[:, :, :, 0], axis=1)) * 0.25
    along_z = restrict_z(jnp.sum(split_major(faces[2]), axis=(1, 3)), even_only=True) * 0.25
    return [along_x, along_y, along_z]


def coarse_tiles(coarse, tiles_dev):
    half_cells = coarse.shape[0]
    shaped = coarse.reshape(coarse.shape[0], coarse.shape[1], tiles_dev, half_cells)
    return shaped.transpose(2, 1, 0, 3).reshape(tiles_dev, half_cells, half_cells * half_cells)


def send_slots(owner_row, device_x, devices_x, tiles_dev):
    mine = lax.dynamic_slice_in_dim(owner_row, device_x * tiles_dev, tiles_dev)
    tile_index = jnp.arange(tiles_dev, dtype=jnp.int32)
    earlier = tile_index[None, :] < tile_index[:, None]
    same_owner = mine[None, :] == mine[:, None]
    order_rank = jnp.sum((earlier & same_owner).astype(jnp.int32), axis=1)
    slot_index = jnp.arange(devices_x * SIDE, dtype=jnp.int32)
    target = slot_index // SIDE
    within = slot_index % SIDE
    matches = (mine[None, :] == target[:, None]) & (order_rank[None, :] == within[:, None])
    picked = jnp.sum(jnp.where(matches, tile_index[None, :], 0), axis=1)
    used = jnp.any(matches, axis=1)
    return (picked, used)


def receive_slots(owner_row, device_x, tiles_dev):
    owned = owner_row == device_x
    tile_ids = jnp.arange(owner_row.shape[0], dtype=jnp.int32)
    position = jnp.cumsum(owned.astype(jnp.int32)) - 1
    wanted = jnp.arange(tiles_dev, dtype=jnp.int32)
    selected = owned[None, :] & (position[None, :] == wanted[:, None])
    chosen_id = jnp.sum(jnp.where(selected, tile_ids[None, :], 0), axis=1)
    source = chosen_id // tiles_dev
    before = jnp.sum(
        (owned[None, :] & (tile_ids[None, :] < (source * tiles_dev)[:, None])).astype(jnp.int32),
        axis=1,
    )
    return source * SIDE + wanted - before


def pack_tiles(tiles, picked, used):
    gathered = jnp.take(tiles, picked, axis=1)
    return jnp.where(used[None, :, None, None], gathered, 0.0)


def local(right_side, alpha_coef, face_coef, owner_map):
    cells = right_side.shape[0]
    tiles_dev = right_side.shape[2] // cells
    devices_x = lax.axis_size("gx")
    device_x = lax.axis_index("gx")
    owner_row = owner_map[0]
    picked, used = send_slots(owner_row, device_x, devices_x, tiles_dev)
    arrival = receive_slots(owner_row, device_x, tiles_dev)
    fields = [average_cells(alpha_coef)] + average_faces(face_coef)
    coef_tiles = jnp.stack([coarse_tiles(field, tiles_dev) for field in fields], axis=0)
    coef_send = pack_tiles(coef_tiles, picked, used)
    solution, residual = smooth_each(right_side, alpha_coef, face_coef)
    residual_tiles = coarse_tiles(average_cells(residual), tiles_dev)[None]
    residual_send = pack_tiles(residual_tiles, picked, used)
    residual_back, coef_back = (
        lax.all_to_all(residual_send, "gx", split_axis=1, concat_axis=1, tiled=True),
        lax.all_to_all(coef_send, "gx", split_axis=1, concat_axis=1, tiled=True),
    )
    coarse_residual = jnp.take(residual_back[0], arrival, axis=0)
    coarse_coef = jnp.take(coef_back, arrival, axis=1)
    return (solution, coarse_residual, coarse_coef)


def solution(mesh):
    return jax.shard_map(
        local,
        mesh=mesh,
        in_specs=(
            P("gx", "gy", None),
            P("gx", "gy", None),
            P(None, "gx", "gy", None),
            P("gy", None),
        ),
        out_specs=(P("gx", "gy", None), P("gx", "gy", None), P(None, "gx", "gy", None)),
        check_vma=False,
    )
```
